256 devices in a mesh: src: 16 (over y, z_lo), snk: 16 (over x, z_hi, core).
Axes of the slice: x: 4, y: 4, z: 8 (z_hi: 2, z_lo: 4; z = z_hi * 4 + z_lo), core: 2. Of those that a mesh axis runs over, the one named last changes fastest.
Arguments:
- perambulator: bfloat16 [16, 16, 2, 512, 512], P('src', 'snk'), may hold values from -0.375 to 0.375
- meson_field: bfloat16 [16, 27, 2, 128, 128], P('snk', None, None, 'src'), may hold values from -0.5 to 0.5
- op_momentum: int32 [4], replicated, may hold values from 0 to 26
- op_gamma: int32 [4], replicated, may hold values from 0 to 15
Outputs:
- loops: float32 [512, 16, 4, 2, 512], P('snk', 'src')
The draws below stay inside these ranges and needn't reach their ends.
Inputs may be any that keep to these rules, and one draw needn't show every extreme that they name: `op_momentum`: index into the momenta of the meson-field table. `op_gamma`: index n of Gamma_n.
All inputs are finite; a program needn't handle non-finite values.
Results may differ from the reference program's by a relative error of at most 0.0029.
Values may be sent and summed in bfloat16 or wider, within the bound.
A program may use at most 64 MiB of HBM per device.

```python
import jax
import jax.numpy as jnp
import numpy as np
from jax import lax

MODES = 128
SPINS = 4
NSM = 512
MOMENTA = 27
K_OPS = 4
NT = 16


def touch_ends(result, own_key, smallest, high):
    longest = result.shape.index(max(result.shape))
    spots = []
    for shift in (0, 1):
        where = [jax.random.randint(jax.random.fold_in(own_key, axis), (), 0, length) for axis, length in enumerate(result.shape)]
        where[longest] = (where[longest] + shift) % result.shape[longest]
        spots.append(tuple(where))
    return result.at[spots[0]].set(smallest).at[spots[1]].set(high)


def with_spikes(values, rng, source, target, shards_of, factor):
    owner, partner = [(jnp.arange(values.shape[dim]) // (values.shape[dim] // shards_of)).reshape([-1 if axis == dim else 1 for axis in range(values.ndim)]) for dim in (source, target)]
    chosen = jax.random.permutation(rng, shards_of)[partner]
    strong = (owner == chosen) | (owner == (partner + shards_of // 2) % shards_of)
    return jnp.where(strong, factor * values, values)


def level_of(key, dims, shards, smallest, top_value):
    gain, own = 1.0, jax.random.fold_in(key, 6)
    for position, parts in shards:
        draws = jnp.exp(jax.random.uniform(jax.random.fold_in(own, position), (parts,), jnp.float32, smallest / len(shards), top_value / len(shards)))
        gain = gain * jnp.repeat(draws, dims[position] // parts).reshape([-1 if axis == position else 1 for axis in range(len(dims))])
    return gain


def centred(rng, shape, spread, reach, pieces=(), kind=jnp.bfloat16):
    entries = spread * jax.random.normal(rng, shape, jnp.float32)
    if pieces:
        entries = entries * level_of(rng, shape, pieces, -0.22, 0.18)
    return jnp.clip(entries, -reach, reach).astype(kind)


def noise_with(key, shape, width, bound, pieces, heavy, kind=jnp.bfloat16):
    values = width * jax.random.normal(key, shape, jnp.float32)
    if pieces:
        values = values * level_of(key, shape, pieces, -0.22, 0.18)
    return jnp.clip(with_spikes(values, jax.random.fold_in(key, 3), *heavy), -bound, bound).astype(kind)


def setup_inputs(seed: int = 0) -> dict:
    keys = jax.random.split(jax.random.key(seed), 5)
    return {
        "perambulator": noise_with(keys[0], (NT, NT, 2, NSM, NSM), NSM ** -0.5, 0.375, ((0, 16), (1, 16)), (1, 3, 16, 2.0)),
        "meson_field": centred(keys[1], (NT, MOMENTA, 2, MODES, MODES), MODES ** -0.5, 0.5, ((0, 16), (3, 16))),
        "op_momentum": touch_ends(jax.random.randint(keys[2], (K_OPS,), 0, MOMENTA), jax.random.fold_in(keys[2], 1), 0, MOMENTA - 1).astype(jnp.int32),
        "op_gamma": touch_ends(jax.random.randint(keys[3], (K_OPS,), 0, 16), jax.random.fold_in(keys[3], 1), 0, 15).astype(jnp.int32),
    }


def gamma_table():
    zero_block = np.zeros((4, 4))
    basis_list = [
        (zero_block, np.array([[0, 0, 0, 1], [0, 0, 1, 0], [0, -1, 0, 0], [-1, 0, 0, 0]], dtype=float)),
        (np.array([[0, 0, 0, -1], [0, 0, 1, 0], [0, 1, 0, 0], [-1, 0, 0, 0]], dtype=float), zero_block),
        (zero_block, np.array([[0, 0, 1, 0], [0, 0, 0, -1], [-1, 0, 0, 0], [0, 1, 0, 0]], dtype=float)),
        (np.array([[0, 0, 1, 0], [0, 0, 0, 1], [1, 0, 0, 0], [0, 1, 0, 0]], dtype=float), zero_block),
    ]
    real_list = []
    imag_list = []
    for number in range(16):
        mat_re = np.eye(4)
        mat_im = np.zeros((4, 4))
        for bit_index in range(4):
            if (number >> bit_index) & 1:
                other_re, other_im = basis_list[bit_index]
                mat_re, mat_im = mat_re @ other_re - mat_im @ other_im, mat_re @ other_im + mat_im @ other_re
        real_list.append(mat_re)
        imag_list.append(mat_im)
    return np.stack(real_list), np.stack(imag_list)


def reference(perambulator, meson_field, op_momentum, op_gamma):
    gamma_re, gamma_im = gamma_table()
    spin_sign = gamma_re[15][[0, 1, 2, 3], [0, 1, 2, 3]]
    column_sign = jnp.asarray(np.repeat(spin_sign, MODES), jnp.float32)
    outer_sign = column_sign[:, None] * column_sign[None, :]
    pick_re = jnp.asarray(gamma_re, jnp.float32)[op_gamma]
    pick_im = jnp.asarray(gamma_im, jnp.float32)[op_gamma]
    spin_modes = SPINS * MODES
    highest = lax.Precision.HIGHEST

    def pair_term(source_slot, sink_slot):
        forward = perambulator[source_slot, sink_slot].astype(jnp.float32).reshape(2, spin_modes, SPINS, MODES)
        fields = meson_field[sink_slot][op_momentum].astype(jnp.float32)
        y_re = jnp.einsum("rsm,kst->krtm", forward[0], pick_re, precision=highest) - jnp.einsum("rsm,kst->krtm", forward[1], pick_im, precision=highest)
        y_im = jnp.einsum("rsm,kst->krtm", forward[0], pick_im, precision=highest) + jnp.einsum("rsm,kst->krtm", forward[1], pick_re, precision=highest)
        a_re = jnp.einsum("krtm,kmn->krtn", y_re, fields[:, 0], precision=highest) - jnp.einsum("krtm,kmn->krtn", y_im, fields[:, 1], precision=highest)
        a_im = jnp.einsum("krtm,kmn->krtn", y_re, fields[:, 1], precision=highest) + jnp.einsum("krtm,kmn->krtn", y_im, fields[:, 0], precision=highest)
        round_re, round_im = lax.optimization_barrier((a_re.astype(jnp.bfloat16), a_im.astype(jnp.bfloat16)))
        front_re = round_re.astype(jnp.float32).reshape(K_OPS, spin_modes, spin_modes)
        front_im = round_im.astype(jnp.float32).reshape(K_OPS, spin_modes, spin_modes)
        backward = perambulator[sink_slot, source_slot].astype(jnp.float32)
        back_re = outer_sign * backward[0].T
        back_im = -outer_sign * backward[1].T
        loop_re = jnp.einsum("krq,qc->rkc", front_re, back_re, precision=highest) - jnp.einsum("krq,qc->rkc", front_im, back_im, precision=highest)
        loop_im = jnp.einsum("krq,qc->rkc", front_re, back_im, precision=highest) + jnp.einsum("krq,qc->rkc", front_im, back_re, precision=highest)
        return jnp.stack([loop_re, loop_im], axis=2)

    def source_row(source_slot):
        def add_sink(carry, sink_slot):
            return carry + pair_term(source_slot, sink_slot), None

        initial = jnp.zeros((spin_modes, K_OPS, 2, spin_modes), jnp.float32)
        return lax.scan(add_sink, initial, jnp.arange(NT, dtype=jnp.int32))[0]

    per_source = lax.map(source_row, jnp.arange(NT, dtype=jnp.int32))
    return jnp.moveaxis(per_source, 0, 1)
```

```python
import jax
import jax.numpy as jnp
import numpy as np
from jax import lax
from jax.experimental import pallas as pl
from jax.experimental.pallas import tpu as pltpu
from jax.sharding import PartitionSpec as P

MESH = pl.DeviceIdType.MESH
NX, NY, NZ = 4, 4, 8
CHUNKS = 4
BF, F32 = jnp.bfloat16, jnp.float32


def gamma_table():
    zero = np.zeros((4, 4))
    basis = [
        (zero, np.array([[0, 0, 0, 1], [0, 0, 1, 0], [0, -1, 0, 0], [-1, 0, 0, 0]], dtype=float)),
        (np.array([[0, 0, 0, -1], [0, 0, 1, 0], [0, 1, 0, 0], [-1, 0, 0, 0]], dtype=float), zero),
        (zero, np.array([[0, 0, 1, 0], [0, 0, 0, -1], [-1, 0, 0, 0], [0, 1, 0, 0]], dtype=float)),
        (np.array([[0, 0, 1, 0], [0, 0, 0, 1], [1, 0, 0, 0], [0, 1, 0, 0]], dtype=float), zero),
    ]
    table = []
    for number in range(16):
        mat = np.eye(4, dtype=complex)
        for bit in range(4):
            if number >> bit & 1:
                mat = mat @ (basis[bit][0] + 1j * basis[bit][1])
        table.append(mat)
    return np.stack(table)


def spin_table():
    table = gamma_table()
    g5 = np.real(np.diagonal(table[15]))
    rows = np.argmax(np.abs(table), axis=1)
    entry = np.take_along_axis(table, rows[:, None, :], axis=1)[:, 0, :] * g5[None, :]
    flat = np.stack([rows, np.real(entry), np.imag(entry)]).round().astype(np.int32)
    return flat.reshape(3 * 64)


def place(x, y, z, c):
    return (y * 4 + z % 4, x * 4 + (z // 4) * 2 + c)


def kernel(gam, mom, tab, tau, mes, out, field, field_b, half, half_b, mir, front, turn, mine, xs, xr, keep, zs, zr,
           s_loc, s_half, r_half, s_f1, r_f1, s_f2, r_f2, s_f3, r_f3, s_mir, r_mir, s_fwd, r_fwd,
           s_x, r_x, s_z, r_z):
    src, snk = lax.axis_index("src"), lax.axis_index("snk")
    x, y, zh, zl, c = snk // 4, src // 4, (snk // 2) % 2, src % 4, snk % 2
    z = zh * 4 + zl
    l1, l0 = zl // 2, zl % 2
    other = 1 - c
    partner = place(x, y, z, other)
    mirror = place(y, x, l1 * 4 + zh * 2 + c, l0)
    own_mirror = (mirror[0] == src) & (mirror[1] == snk)
    far_mirror = jnp.logical_not(own_mirror)
    zl_peers = [place(x, y, zh * 4 + (zl + d) % 4, c) for d in (1, 2, 3)]
    y_peers = [place(x, (y + d) % 4, z, c) for d in (1, 2, 3)]
    x_peers = [place((x + d) % 4, y, z, c) for d in (1, 2, 3)]
    z_peer = place(x, y, (z + 4) % 8, c)

    bar = pltpu.get_barrier_semaphore()
    for dev in [partner, z_peer, *zl_peers, *y_peers, *x_peers]:
        pl.semaphore_signal(bar, inc=1, device_id=dev, device_id_type=MESH)

    @pl.when(far_mirror)
    def _():
        pl.semaphore_signal(bar, inc=1, device_id=mirror, device_id_type=MESH)

    for k in range(4):
        field[k, :, src] = mes[0, mom[k]]
    local = [
        pltpu.make_async_copy(
            tau.at[p, :, c, :, s * 128 : (s + 1) * 128], half.at[p, s], s_loc.at[p, s]
        )
        for p in range(2)
        for s in range(4)
    ]
    for cp in local:
        cp.start()

    pl.semaphore_wait(bar, jnp.where(far_mirror, 12, 11))

    def send(a, b, ss, rs, dev):
        return pltpu.make_async_remote_copy(
            src_ref=a, dst_ref=b, send_sem=ss, recv_sem=rs, device_id=dev, device_id_type=MESH
        )

    f1 = [
        send(field.at[:, :, src], field.at[:, :, src], s_f1.at[d], r_f1.at[d], zl_peers[d])
        for d in range(3)
    ]
    for cp in f1:
        cp.start()
    swap = [
        send(
            tau.at[p, :, other, :, s * 128 : (s + 1) * 128],
            half_b.at[p, s],
            s_half.at[p, s],
            r_half.at[p, s],
            partner,
        )
        for p in range(2)
        for s in range(4)
    ]
    for cp in swap:
        cp.start()
    mcopy = [
        send(tau.at[:, pl.ds(2 * j, 2)], mir.at[0, j], s_mir.at[j], r_mir.at[j], mirror)
        for j in range(CHUNKS)
    ]
    mlocal = [
        pltpu.make_async_copy(tau.at[:, pl.ds(2 * j, 2)], mir.at[0, j], r_mir.at[j])
        for j in range(CHUNKS)
    ]

    @pl.when(far_mirror)
    def _():
        for cp in mcopy:
            cp.start()

    @pl.when(own_mirror)
    def _():
        for cp in mlocal:
            cp.start()

    for d in range(3):
        send(field.at[:, :, src], field.at[:, :, src], s_f1.at[d], r_f1.at[d], zl_peers[d]).wait_recv()
    rows = field.at[:, :, pl.ds(4 * y, 4)]
    f2 = [send(rows, rows, s_f2.at[d], r_f2.at[d], y_peers[d]) for d in range(3)]
    for cp in f2:
        cp.start()
    for cp in f2:
        cp.wait_recv()
    f3 = send(field, field_b, s_f3, r_f3, partner)
    f3.start()
    for cp in local:
        cp.wait()

    def make_front(b, field, half):
        def for_op(k, carry):
            gamma = gam[k]
            m_re = field[k, 0].astype(F32).reshape(128, 128)
            m_im = field[k, 1].astype(F32).reshape(128, 128)
            for t in range(4):
                spin = tab[gamma * 4 + t]
                g_re = tab[64 + gamma * 4 + t].astype(F32)
                g_im = tab[128 + gamma * 4 + t].astype(F32)
                top = (g_re * m_re - g_im * m_im).astype(BF)
                low = (g_re * m_im + g_im * m_re).astype(BF)
                mix = jnp.concatenate(
                    [jnp.concatenate([top, low], axis=1), jnp.concatenate([-low, top], axis=1)], axis=0
                )
                left = jnp.concatenate(
                    [half[0, spin].reshape(256, 128), half[1, spin].reshape(256, 128)], axis=1
                )
                made = jnp.dot(left, mix, preferred_element_type=F32).astype(BF)
                made = made.reshape(4, 2, 32, 256)
                front[b, 0, :, :, k, :, t * 128 : (t + 1) * 128] = made[..., :128]
                front[b, 1, :, :, k, :, t * 128 : (t + 1) * 128] = made[..., 128:]
            return carry

        lax.fori_loop(0, 4, for_op, 0)

    make_front(0, field, half)
    f3.wait_recv()
    for cp in swap:
        cp.wait_recv()
    make_front(1, field_b, half_b)

    def x_copy(j, d):
        return send(xs.at[j, d], xr.at[j, d], s_x.at[j, d], r_x.at[j, d], x_peers[d])

    def z_copy(j):
        return send(zs.at[j], zr.at[j], s_z.at[j], r_z.at[j], z_peer)

    def product(j):
        for b in (0, 1):
            re = mir[b, j, 0].reshape(128, 512)
            im = mir[b, j, 1].reshape(128, 512)
            if j >= 2:
                re, im = -re, -im
            turn[b, 0] = jnp.concatenate([re, -im], axis=0).T
            turn[b, 1] = jnp.concatenate([im, re], axis=0).T

        def part(row):
            total = jnp.zeros((256, 256), F32)
            for b in (0, 1):
                for p in (0, 1):
                    total += jnp.dot(
                        front[b, p, row].reshape(256, 512), turn[b, p], preferred_element_type=F32
                    )
            return total

        for d in (1, 0, 2):
            xs[j, d] = part((x + d + 1) % 4).astype(BF)
            x_copy(j, d).start()
        mine[j] = part(x)

    def over_x(j):
        for d in range(3):
            x_copy(j, d).wait_recv()

        def rows_of(which):
            at = pl.ds(pl.multiple_of(which * 128, 128), 128)
            total = mine[j, at]
            for d in range(3):
                total += xr[j, d, at].astype(F32)
            return total

        zs[j] = rows_of(1 - zh).astype(BF)
        z_copy(j).start()
        keep[j] = rows_of(zh)

    def over_z(j):
        z_copy(j).wait_recv()
        total = (keep[j] + zr[j].astype(F32)).reshape(4, 32, 256)
        for p in (0, 1):
            out[:, p, :, j * 128 : (j + 1) * 128] = total[..., p * 128 : (p + 1) * 128]

    def fwd(j):
        return send(mir.at[0, j], mir.at[1, j], s_fwd.at[j], r_fwd.at[j], partner)

    def arrive(j):
        mlocal[j].wait()
        fwd(j).start()

    for j in range(CHUNKS):
        arrive(j)
        fwd(j).wait_recv()
        product(j)
        if j >= 1:
            over_x(j - 1)
        if j >= 2:
            over_z(j - 2)
    over_x(CHUNKS - 1)
    over_z(CHUNKS - 2)
    over_z(CHUNKS - 1)

    for cp in [*f1, *f2, f3, *swap]:
        cp.wait_send()

    @pl.when(far_mirror)
    def _():
        for cp in mcopy:
            cp.wait_send()

    for j in range(CHUNKS):
        fwd(j).wait_send()
        for d in range(3):
            x_copy(j, d).wait_send()
        z_copy(j).wait_send()


def on_device(perambulator, meson_field, op_momentum, op_gamma):
    tau = perambulator.reshape(2, 8, 2, 32, 512)
    tab = jnp.asarray(spin_table())
    smem = pl.BlockSpec(memory_space=pltpu.SMEM)
    vmem = pl.BlockSpec(memory_space=pltpu.VMEM)
    dma = pltpu.SemaphoreType.DMA
    loops = pl.pallas_call(
        kernel,
        out_shape=jax.ShapeDtypeStruct((4, 2, 32, 512), F32),
        in_specs=[smem, smem, smem, pl.BlockSpec(memory_space=pl.ANY), vmem],
        out_specs=vmem,
        scratch_shapes=[
            pltpu.VMEM((4, 2, 16, 8, 128), BF),
            pltpu.VMEM((4, 2, 16, 8, 128), BF),
            pltpu.VMEM((2, 4, 8, 32, 128), BF),
            pltpu.VMEM((2, 4, 8, 32, 128), BF),
            pltpu.VMEM((2, CHUNKS, 2, 2, 2, 32, 512), BF),
            pltpu.VMEM((2, 2, 4, 2, 4, 32, 512), BF),
            pltpu.VMEM((2, 2, 512, 256), BF),
            pltpu.VMEM((CHUNKS, 256, 256), F32),
            pltpu.VMEM((CHUNKS, 3, 256, 256), BF),
            pltpu.VMEM((CHUNKS, 3, 256, 256), BF),
            pltpu.VMEM((CHUNKS, 128, 256), F32),
            pltpu.VMEM((CHUNKS, 128, 256), BF),
            pltpu.VMEM((CHUNKS, 128, 256), BF),
            dma((2, 4)), dma((2, 4)), dma((2, 4)), dma((3,)), dma((3,)), dma((3,)), dma((3,)), dma(()), dma(()),
            dma((CHUNKS,)), dma((CHUNKS,)), dma((CHUNKS,)), dma((CHUNKS,)),
            dma((CHUNKS, 3)), dma((CHUNKS, 3)), dma((CHUNKS,)), dma((CHUNKS,)),
        ],
        compiler_params=pltpu.CompilerParams(
            collective_id=0, has_side_effects=True, vmem_limit_bytes=48 * 1024 * 1024
        ),
        name="loops",
    )(op_gamma, op_momentum, tab, tau, meson_field)
    return jnp.transpose(loops, (2, 0, 1, 3)).reshape(32, 1, 4, 2, 512)


def solution(mesh):
    return jax.shard_map(
        on_device,
        mesh=mesh,
        in_specs=(P("src", "snk"), P("snk", None, None, "src"), P(), P()),
        out_specs=P("snk", "src"),
        check_vma=False,
    )
```

```python
import jax
import jax.numpy as jnp
import numpy as np
from jax import lax
from jax.experimental import pallas as pl
from jax.experimental.pallas import tpu as pltpu
from jax.sharding import PartitionSpec as P

MESH = pl.DeviceIdType.MESH
NX, NY, NZ = 4, 4, 8
CHUNKS = 4
LONG = (1, 3)
BF, F32 = jnp.bfloat16, jnp.float32


def gamma_table():
    zero = np.zeros((4, 4))
    basis = [
        (zero, np.array([[0, 0, 0, 1], [0, 0, 1, 0], [0, -1, 0, 0], [-1, 0, 0, 0]], dtype=float)),
        (np.array([[0, 0, 0, -1], [0, 0, 1, 0], [0, 1, 0, 0], [-1, 0, 0, 0]], dtype=float), zero),
        (zero, np.array([[0, 0, 1, 0], [0, 0, 0, -1], [-1, 0, 0, 0], [0, 1, 0, 0]], dtype=float)),
        (np.array([[0, 0, 1, 0], [0, 0, 0, 1], [1, 0, 0, 0], [0, 1, 0, 0]], dtype=float), zero),
    ]
    table = []
    for number in range(16):
        mat = np.eye(4, dtype=complex)
        for bit in range(4):
            if number >> bit & 1:
                mat = mat @ (basis[bit][0] + 1j * basis[bit][1])
        table.append(mat)
    return np.stack(table)


def spin_table():
    table = gamma_table()
    g5 = np.real(np.diagonal(table[15]))
    rows = np.argmax(np.abs(table), axis=1)
    entry = np.take_along_axis(table, rows[:, None, :], axis=1)[:, 0, :] * g5[None, :]
    flat = np.stack([rows, np.real(entry), np.imag(entry)]).round().astype(np.int32)
    return flat.reshape(3 * 64)


def place(x, y, z, c):
    return (y * 4 + z % 4, x * 4 + (z // 4) * 2 + c)


def goes_around(z, c):
    return (z == 2) | (z == 5) | ((z == 3) & (c == 1)) | ((z == 4) & (c == 0))


def kernel(gam_in, mom_in, tab_in, tau, mes_in, out, gam, mom, tab, mes, field, field_b, half, half_b, mir, front, turn, mine, xs, xr, keep, zs, zr, ybuf, wbuf, turned,
           s_loc, s_half, r_half, s_f1, r_f1, s_f2, r_f2, s_f3, r_f3, s_mir, r_mir, s_fwd, r_fwd,
           s_x, r_x, s_z, r_z, s_y, r_y, s_w, r_w, s_t, r_t):
    src, snk = lax.axis_index("src"), lax.axis_index("snk")
    x, y, zh, zl, c = snk // 4, src // 4, (snk // 2) % 2, src % 4, snk % 2
    z = zh * 4 + zl
    l1, l0 = zl // 2, zl % 2
    other = 1 - c
    partner = place(x, y, z, other)
    zm, cm = l1 * 4 + zh * 2 + c, l0
    across = place(y, x, z, c)
    around, around_in = goes_around(z, c), goes_around(zm, cm)
    end = (z == 0) | (z == 7)
    end_two = ((z == 7) & (c == 0)) | ((z == 0) & (c == 1))
    w_slot = jnp.where((z == 2) | (z == 5), 0, 1)
    up = z == 7
    w_ends = (
        (end, place(x, y, jnp.where(up, 2, 5), c), place(x, y, jnp.where(up, 4 + c, 2 + c), jnp.where(up, 0, 1))),
        (end_two, place(x, y, jnp.where(up, 4, 3), c), place(x, y, jnp.where(up, 2, 5), jnp.where(up, 0, 1))),
    )
    diag, off = x == y, x != y
    stays = (z == zm) & (c == cm)
    moves = jnp.logical_not(stays)
    z_mirror = place(x, y, zm, cm)
    far_relay = place(x, y, 7 * (1 - z % 2), c)
    far_relay_in = place(x, y, 7 * (1 - zm % 2), cm)

    def behind(i):
        return (y + 4 - i) % 4

    def relays(i):
        return x != behind(i)

    zl_peers = [place(x, y, zh * 4 + (zl + d) % 4, c) for d in (1, 2, 3)]
    y_peers = [place(x, (y + d) % 4, z, c) for d in (1, 2, 3)]
    x_peers = [place((x + d) % 4, y, z, c) for d in (1, 2, 3)]
    z_peer = place(x, y, (z + 4) % 8, c)

    pltpu.make_async_copy(mes_in, mes, s_loc.at[1, 3]).start()
    pltpu.make_async_copy(gam_in, gam, s_loc.at[0, 0]).start()
    pltpu.make_async_copy(mom_in, mom, s_loc.at[0, 1]).start()
    pltpu.make_async_copy(tab_in, tab, s_loc.at[0, 2]).start()
    bar = pltpu.get_barrier_semaphore()
    for dev in [partner, z_peer, *zl_peers, *y_peers, *x_peers]:
        pl.semaphore_signal(bar, inc=1, device_id=dev, device_id_type=MESH)

    def greet(cond, *devs):
        @pl.when(cond)
        def _():
            for dev in devs:
                pl.semaphore_signal(bar, inc=1, device_id=dev, device_id_type=MESH)

        return jnp.where(cond, len(devs), 0)

    peers = 11
    peers += greet(off, across)
    for i in (1, 2, 3):
        peers += greet(relays(i), place(behind(i), x, z, c))
        peers += greet(off, place(y, (x + i) % 4, z, c))
    peers += greet(moves, z_mirror)
    peers += greet(around, far_relay)
    peers += greet(around_in, far_relay_in)
    for cond, dev_from, dev_to in w_ends:
        peers += greet(cond, dev_from, dev_to)

    pltpu.make_async_copy(mes_in, mes, s_loc.at[1, 3]).wait()
    pltpu.make_async_copy(gam_in, gam, s_loc.at[0, 0]).wait()
    pltpu.make_async_copy(mom_in, mom, s_loc.at[0, 1]).wait()
    pltpu.make_async_copy(tab_in, tab, s_loc.at[0, 2]).wait()
    for k in range(4):
        field[k, :, src] = mes[0, mom[k]]
    local = [
        pltpu.make_async_copy(
            tau.at[p, :, c, :, s * 128 : (s + 1) * 128], half.at[p, s], s_loc.at[p, s]
        )
        for p in range(2)
        for s in range(4)
    ]
    for cp in local:
        cp.start()

    pl.semaphore_wait(bar, peers)

    def send(a, b, ss, rs, dev):
        return pltpu.make_async_remote_copy(
            src_ref=a, dst_ref=b, send_sem=ss, recv_sem=rs, device_id=dev, device_id_type=MESH
        )

    f1 = [
        send(field.at[:, :, src], field.at[:, :, src], s_f1.at[d], r_f1.at[d], zl_peers[d])
        for d in range(3)
    ]
    for cp in f1:
        cp.start()
    swap = [
        send(
            tau.at[p, :, other, :, s * 128 : (s + 1) * 128],
            half_b.at[p, s],
            s_half.at[p, s],
            r_half.at[p, s],
            partner,
        )
        for p in range(2)
        for s in range(4)
    ]
    for cp in swap:
        cp.start()
    def rows(j, i):
        return tau.at[:, 2 * j + i // 2, i % 2]

    def landed(ref, sem):
        pltpu.make_async_copy(ref, ref, sem).wait()

    def to_relay(j, i):
        dev = place(x, (y + i) % 4, z, c)
        return send(rows(j, i), ybuf.at[j, i - 1], s_mir.at[j, i], r_y.at[j, i - 1], dev)

    def step_across(j, i, final):
        dst, sem = (mir.at[0, j, i], r_mir.at[j, i]) if final else (turned.at[j, i], r_t.at[j, i])
        if i == 0:
            return send(rows(j, 0), dst, s_mir.at[j, 0], sem, across)
        dev = place(behind(i), x, z, c)
        return send(ybuf.at[j, i - 1], dst, s_y.at[j, i - 1], sem, dev)

    def along_z(j, i, ref):
        return send(ref, mir.at[0, j, i], s_t.at[j, i], r_mir.at[j, i], z_mirror)

    def to_far_relay(j, i, ref):
        return send(ref, wbuf.at[j, i // 2, w_slot], s_t.at[j, i], r_w.at[j, i // 2, w_slot], far_relay)

    def from_far_relay(j, i, e):
        k = i // 2
        return send(wbuf.at[j, k, e], mir.at[0, j, i], s_w.at[j, k, e], r_mir.at[j, i], w_ends[e][2])

    def local_piece(j, i):
        return pltpu.make_async_copy(rows(j, i), mir.at[0, j, i], r_mir.at[j, i])

    def start_z(j, i, ref):
        if i in LONG:

            @pl.when(around)
            def _():
                to_far_relay(j, i, ref).start()

            @pl.when(jnp.logical_not(around))
            def _():
                along_z(j, i, ref).start()
        else:
            along_z(j, i, ref).start()

    def stage_a(j):
        @pl.when(off)
        def _():
            for i in (1, 3, 2):
                to_relay(j, i).start()

        @pl.when(diag & moves)
        def _():
            for i in (1, 3, 0, 2):
                start_z(j, i, rows(j, i))

        @pl.when(diag & stays)
        def _():
            for i in range(4):
                local_piece(j, i).start()

    def stage_b(j):
        def go(i):
            @pl.when(stays)
            def _():
                step_across(j, i, True).start()

            @pl.when(moves)
            def _():
                step_across(j, i, False).start()

        @pl.when(off)
        def _():
            go(0)

        for i in (1, 3, 2):

            @pl.when(relays(i))
            def _():
                landed(ybuf.at[j, i - 1], r_y.at[j, i - 1])
                go(i)

    def stage_c(j):
        @pl.when(off & moves)
        def _():
            for i in (0, 1, 3, 2):
                landed(turned.at[j, i], r_t.at[j, i])
                start_z(j, i, turned.at[j, i])

    def stage_w(j):
        for e in range(2):

            @pl.when(w_ends[e][0])
            def _():
                for i in LONG:
                    landed(wbuf.at[j, i // 2, e], r_w.at[j, i // 2, e])
                    from_far_relay(j, i, e).start()

    for j in range(CHUNKS):
        stage_a(j)

    for d in range(3):
        send(field.at[:, :, src], field.at[:, :, src], s_f1.at[d], r_f1.at[d], zl_peers[d]).wait_recv()
    mine_y = field.at[:, :, pl.ds(4 * y, 4)]
    f2 = [send(mine_y, mine_y, s_f2.at[d], r_f2.at[d], y_peers[d]) for d in range(3)]
    for cp in f2:
        cp.start()
    for cp in f2:
        cp.wait_recv()
    f3 = send(field, field_b, s_f3, r_f3, partner)
    f3.start()
    for cp in local:
        cp.wait()

    def make_front(b, field, half):
        def for_op(k, carry):
            gamma = gam[k]
            m_re = field[k, 0].astype(F32).reshape(128, 128)
            m_im = field[k, 1].astype(F32).reshape(128, 128)
            for t in range(4):
                spin = tab[gamma * 4 + t]
                g_re = tab[64 + gamma * 4 + t].astype(F32)
                g_im = tab[128 + gamma * 4 + t].astype(F32)
                top = (g_re * m_re - g_im * m_im).astype(BF)
                low = (g_re * m_im + g_im * m_re).astype(BF)
                mix = jnp.concatenate(
                    [jnp.concatenate([top, low], axis=1), jnp.concatenate([-low, top], axis=1)], axis=0
                )
                left = jnp.concatenate(
                    [half[0, spin].reshape(256, 128), half[1, spin].reshape(256, 128)], axis=1
                )
                made = jnp.dot(left, mix, preferred_element_type=F32).astype(BF)
                made = made.reshape(4, 2, 32, 256)
                front[b, 0, :, :, k, :, t * 128 : (t + 1) * 128] = made[..., :128]
                front[b, 1, :, :, k, :, t * 128 : (t + 1) * 128] = made[..., 128:]
            return carry

        lax.fori_loop(0, 4, for_op, 0)

    stage_b(0)
    make_front(0, field, half)
    stage_b(1)
    stage_c(0)
    f3.wait_recv()
    for cp in swap:
        cp.wait_recv()
    make_front(1, field_b, half_b)
    stage_b(2)
    stage_c(1)
    stage_w(0)
    def x_copy(j, d):
        return send(xs.at[j, d], xr.at[j, d], s_x.at[j, d], r_x.at[j, d], x_peers[d])

    def z_copy(j):
        return send(zs.at[j], zr.at[j], s_z.at[j], r_z.at[j], z_peer)

    def product(j):
        for b in (0, 1):
            re = mir[b, j, :, 0].reshape(128, 512)
            im = mir[b, j, :, 1].reshape(128, 512)
            if j >= 2:
                re, im = -re, -im
            turn[b, 0] = jnp.concatenate([re, -im], axis=0).T
            turn[b, 1] = jnp.concatenate([im, re], axis=0).T

        def part(row):
            total = jnp.zeros((256, 256), F32)
            for b in (0, 1):
                for p in (0, 1):
                    total += jnp.dot(
                        front[b, p, row].reshape(256, 512), turn[b, p], preferred_element_type=F32
                    )
            return total

        for d in (1, 0, 2):
            xs[j, d] = part((x + d + 1) % 4).astype(BF)
            x_copy(j, d).start()
        mine[j] = part(x)

    def over_x(j):
        for d in range(3):
            x_copy(j, d).wait_recv()

        def rows_of(which):
            at = pl.ds(pl.multiple_of(which * 128, 128), 128)
            total = mine[j, at]
            for d in range(3):
                total += xr[j, d, at].astype(F32)
            return total

        zs[j] = rows_of(1 - zh).astype(BF)
        z_copy(j).start()
        keep[j] = rows_of(zh)

    def over_z(j):
        z_copy(j).wait_recv()
        total = (keep[j] + zr[j].astype(F32)).reshape(4, 32, 256)
        for p in (0, 1):
            out[:, p, :, j * 128 : (j + 1) * 128] = total[..., p * 128 : (p + 1) * 128]

    def fwd(j, q):
        return send(mir.at[0, j, q], mir.at[1, j, q], s_fwd.at[j, q], r_fwd.at[j, q], partner)

    def arrive(j):
        for q in (0, 2, 1, 3):
            local_piece(j, q).wait()
            fwd(j, q).start()

    for j in range(CHUNKS):
        arrive(j)
        for q in (0, 2, 1, 3):
            fwd(j, q).wait_recv()
        product(j)
        if j + 1 < CHUNKS:
            stage_w(j + 1)
        if j == 0:
            stage_b(3)
            stage_c(2)
        if j == 1:
            stage_c(3)
        if j >= 1:
            over_x(j - 1)
        if j >= 2:
            over_z(j - 2)
    over_x(CHUNKS - 1)
    over_z(CHUNKS - 2)
    over_z(CHUNKS - 1)

    for cp in [*f1, *f2, f3, *swap]:
        cp.wait_send()

    for j in range(CHUNKS):

        @pl.when(off)
        def _():
            step_across(j, 0, False).wait_send()
            for i in (1, 2, 3):
                to_relay(j, i).wait_send()

        @pl.when(moves)
        def _():
            for i in range(4):
                along_z(j, i, turned.at[j, i]).wait_send()

        for i in (1, 2, 3):

            @pl.when(relays(i))
            def _():
                step_across(j, i, False).wait_send()

        for e in range(2):

            @pl.when(w_ends[e][0])
            def _():
                for i in LONG:
                    from_far_relay(j, i, e).wait_send()

        for q in range(4):
            fwd(j, q).wait_send()
        for d in range(3):
            x_copy(j, d).wait_send()
        z_copy(j).wait_send()


def on_device(perambulator, meson_field, op_momentum, op_gamma):
    tau = perambulator.reshape(2, 8, 2, 32, 512)
    tab = jnp.asarray(spin_table())
    vmem = pl.BlockSpec(memory_space=pltpu.VMEM)
    dma = pltpu.SemaphoreType.DMA
    loops = pl.pallas_call(
        kernel,
        out_shape=jax.ShapeDtypeStruct((4, 2, 32, 512), F32),
        in_specs=[pl.BlockSpec(memory_space=pl.ANY)] * 5,
        out_specs=vmem,
        scratch_shapes=[
            pltpu.SMEM((4,), jnp.int32),
            pltpu.SMEM((4,), jnp.int32),
            pltpu.SMEM((192,), jnp.int32),
            pltpu.VMEM((1, 27, 2, 8, 128), BF),
            pltpu.VMEM((4, 2, 16, 8, 128), BF),
            pltpu.VMEM((4, 2, 16, 8, 128), BF),
            pltpu.VMEM((2, 4, 8, 32, 128), BF),
            pltpu.VMEM((2, 4, 8, 32, 128), BF),
            pltpu.VMEM((2, CHUNKS, 4, 2, 32, 512), BF),
            pltpu.VMEM((2, 2, 4, 2, 4, 32, 512), BF),
            pltpu.VMEM((2, 2, 512, 256), BF),
            pltpu.VMEM((CHUNKS, 256, 256), F32),
            pltpu.VMEM((CHUNKS, 3, 256, 256), BF),
            pltpu.VMEM((CHUNKS, 3, 256, 256), BF),
            pltpu.VMEM((CHUNKS, 128, 256), F32),
            pltpu.VMEM((CHUNKS, 128, 256), BF),
            pltpu.VMEM((CHUNKS, 128, 256), BF),
            pltpu.VMEM((CHUNKS, 3, 2, 32, 512), BF),
            pltpu.VMEM((CHUNKS, 2, 2, 2, 32, 512), BF),
            pltpu.VMEM((CHUNKS, 4, 2, 32, 512), BF),
            dma((2, 4)), dma((2, 4)), dma((2, 4)), dma((3,)), dma((3,)), dma((3,)), dma((3,)), dma(()), dma(()),
            dma((CHUNKS, 4)), dma((CHUNKS, 4)), dma((CHUNKS, 4)), dma((CHUNKS, 4)),
            dma((CHUNKS, 3)), dma((CHUNKS, 3)), dma((CHUNKS,)), dma((CHUNKS,)),
            dma((CHUNKS, 3)), dma((CHUNKS, 3)), dma((CHUNKS, 2, 2)), dma((CHUNKS, 2, 2)), dma((CHUNKS, 4)), dma((CHUNKS, 4)),
        ],
        compiler_params=pltpu.CompilerParams(
            collective_id=0, has_side_effects=True, vmem_limit_bytes=67_000_000
        ),
        name="loops",
    )(op_gamma, op_momentum, tab, tau, meson_field)
    return jnp.transpose(loops, (2, 0, 1, 3)).reshape(32, 1, 4, 2, 512)


def solution(mesh):
    return jax.shard_map(
        on_device,
        mesh=mesh,
        in_specs=(P("src", "snk"), P("snk", None, None, "src"), P(), P()),
        out_specs=P("snk", "src"),
        check_vma=False,
    )
```

```python
import jax
import jax.numpy as jnp
import numpy as np
from jax import lax
from jax.experimental import pallas as pl
from jax.experimental.pallas import tpu as pltpu
from jax.sharding import PartitionSpec as P

MESH = pl.DeviceIdType.MESH
NX, NY, NZ = 4, 4, 8
CHUNKS = 4
LONG = (1, 3)
BF, F32 = jnp.bfloat16, jnp.float32


def gamma_table():
    zero = np.zeros((4, 4))
    basis = [
        (zero, np.array([[0, 0, 0, 1], [0, 0, 1, 0], [0, -1, 0, 0], [-1, 0, 0, 0]], dtype=float)),
        (np.array([[0, 0, 0, -1], [0, 0, 1, 0], [0, 1, 0, 0], [-1, 0, 0, 0]], dtype=float), zero),
        (zero, np.array([[0, 0, 1, 0], [0, 0, 0, -1], [-1, 0, 0, 0], [0, 1, 0, 0]], dtype=float)),
        (np.array([[0, 0, 1, 0], [0, 0, 0, 1], [1, 0, 0, 0], [0, 1, 0, 0]], dtype=float), zero),
    ]
    table = []
    for number in range(16):
        mat = np.eye(4, dtype=complex)
        for bit in range(4):
            if number >> bit & 1:
                mat = mat @ (basis[bit][0] + 1j * basis[bit][1])
        table.append(mat)
    return np.stack(table)


def spin_table():
    table = gamma_table()
    g5 = np.real(np.diagonal(table[15]))
    rows = np.argmax(np.abs(table), axis=1)
    entry = np.take_along_axis(table, rows[:, None, :], axis=1)[:, 0, :] * g5[None, :]
    flat = np.stack([rows, np.real(entry), np.imag(entry)]).round().astype(np.int32)
    return flat.reshape(3 * 64)


def place(x, y, z, c):
    return (y * 4 + z % 4, x * 4 + (z // 4) * 2 + c)


def goes_around(z, c):
    return (z == 2) | (z == 5) | ((z == 3) & (c == 1)) | ((z == 4) & (c == 0))


def kernel(gam_in, mom_in, tab_in, tau, mes_in, out, gam, mom, tab, mes, field, field_b, half, half_b, mir, front, turn, mine, xs, xr, keep, zs, zr, ybuf, wbuf, turned,
           s_loc, s_half, r_half, s_f1, r_f1, s_f2, r_f2, s_f3, r_f3, s_mir, r_mir, s_fwd, r_fwd,
           s_x, r_x, s_z, r_z, s_y, r_y, s_w, r_w, s_t, r_t):
    src, snk = lax.axis_index("src"), lax.axis_index("snk")
    x, y, zh, zl, c = snk // 4, src // 4, (snk // 2) % 2, src % 4, snk % 2
    z = zh * 4 + zl
    l1, l0 = zl // 2, zl % 2
    other = 1 - c
    partner = place(x, y, z, other)
    zm, cm = l1 * 4 + zh * 2 + c, l0
    across = place(y, x, z, c)
    around, around_in = goes_around(z, c), goes_around(zm, cm)
    end = (z == 0) | (z == 7)
    end_two = ((z == 7) & (c == 0)) | ((z == 0) & (c == 1))
    w_slot = jnp.where((z == 2) | (z == 5), 0, 1)
    up = z == 7
    w_ends = (
        (end, place(x, y, jnp.where(up, 2, 5), c), place(x, y, jnp.where(up, 4 + c, 2 + c), jnp.where(up, 0, 1))),
        (end_two, place(x, y, jnp.where(up, 4, 3), c), place(x, y, jnp.where(up, 2, 5), jnp.where(up, 0, 1))),
    )
    diag, off = x == y, x != y
    stays = (z == zm) & (c == cm)
    moves = jnp.logical_not(stays)
    z_mirror = place(x, y, zm, cm)
    far_relay = place(x, y, 7 * (1 - z % 2), c)
    far_relay_in = place(x, y, 7 * (1 - zm % 2), cm)

    def behind(i):
        return (y + 4 - i) % 4

    def relays(i):
        return x != behind(i)

    zl_peers = [place(x, y, zh * 4 + (zl + d) % 4, c) for d in (1, 2, 3)]
    y_peers = [place(x, (y + d) % 4, z, c) for d in (1, 2, 3)]
    x_peers = [place((x + d) % 4, y, z, c) for d in (1, 2, 3)]
    z_peer = place(x, y, (z + 4) % 8, c)

    pltpu.make_async_copy(mes_in, mes, s_loc.at[1, 3]).start()
    pltpu.make_async_copy(gam_in, gam, s_loc.at[0, 0]).start()
    pltpu.make_async_copy(mom_in, mom, s_loc.at[0, 1]).start()
    pltpu.make_async_copy(tab_in, tab, s_loc.at[0, 2]).start()
    bar = pltpu.get_barrier_semaphore()
    for dev in [partner, z_peer, *zl_peers, *y_peers, *x_peers]:
        pl.semaphore_signal(bar, inc=1, device_id=dev, device_id_type=MESH)

    def greet(cond, *devs):
        @pl.when(cond)
        def _():
            for dev in devs:
                pl.semaphore_signal(bar, inc=1, device_id=dev, device_id_type=MESH)

        return jnp.where(cond, len(devs), 0)

    peers = 11
    peers += greet(off, across)
    for i in (1, 2, 3):
        peers += greet(relays(i), place(behind(i), x, z, c))
        peers += greet(off, place(y, (x + i) % 4, z, c))
    peers += greet(moves, z_mirror)
    peers += greet(around, far_relay)
    peers += greet(around_in, far_relay_in)
    for cond, dev_from, dev_to in w_ends:
        peers += greet(cond, dev_from, dev_to)

    pltpu.make_async_copy(mes_in, mes, s_loc.at[1, 3]).wait()
    pltpu.make_async_copy(gam_in, gam, s_loc.at[0, 0]).wait()
    pltpu.make_async_copy(mom_in, mom, s_loc.at[0, 1]).wait()
    pltpu.make_async_copy(tab_in, tab, s_loc.at[0, 2]).wait()
    for k in range(4):
        field[k, :, src] = mes[0, mom[k]]
    local = [
        pltpu.make_async_copy(
            tau.at[p, :, c, :, s * 128 : (s + 1) * 128], half.at[p, s], s_loc.at[p, s]
        )
        for p in range(2)
        for s in range(4)
    ]
    for cp in local:
        cp.start()

    pl.semaphore_wait(bar, peers)

    def send(a, b, ss, rs, dev):
        return pltpu.make_async_remote_copy(
            src_ref=a, dst_ref=b, send_sem=ss, recv_sem=rs, device_id=dev, device_id_type=MESH
        )

    f1 = [
        send(field.at[:, :, src], field.at[:, :, src], s_f1.at[d], r_f1.at[d], zl_peers[d])
        for d in range(3)
    ]
    for cp in f1:
        cp.start()
    swap = [
        send(
            tau.at[p, :, other, :, s * 128 : (s + 1) * 128],
            half_b.at[p, s],
            s_half.at[p, s],
            r_half.at[p, s],
            partner,
        )
        for p in range(2)
        for s in range(4)
    ]
    for cp in swap:
        cp.start()
    def rows(j, i):
        return tau.at[:, 2 * j + i // 2, i % 2]

    def landed(ref, sem):
        pltpu.make_async_copy(ref, ref, sem).wait()

    def to_relay(j, i):
        dev = place(x, (y + i) % 4, z, c)
        return send(rows(j, i), ybuf.at[j, i - 1], s_mir.at[j, i], r_y.at[j, i - 1], dev)

    def step_across(j, i, final):
        dst, sem = (mir.at[0, j, i], r_mir.at[j, i]) if final else (turned.at[j, i], r_t.at[j, i])
        if i == 0:
            return send(rows(j, 0), dst, s_mir.at[j, 0], sem, across)
        dev = place(behind(i), x, z, c)
        return send(ybuf.at[j, i - 1], dst, s_y.at[j, i - 1], sem, dev)

    def along_z(j, i, ref):
        return send(ref, mir.at[0, j, i], s_t.at[j, i], r_mir.at[j, i], z_mirror)

    def to_far_relay(j, i, ref):
        return send(ref, wbuf.at[j, i // 2, w_slot], s_t.at[j, i], r_w.at[j, i // 2, w_slot], far_relay)

    def from_far_relay(j, i, e):
        k = i // 2
        return send(wbuf.at[j, k, e], mir.at[0, j, i], s_w.at[j, k, e], r_mir.at[j, i], w_ends[e][2])

    def local_piece(j, i):
        return pltpu.make_async_copy(rows(j, i), mir.at[0, j, i], r_mir.at[j, i])

    def start_z(j, i, ref):
        if i in LONG:

            @pl.when(around)
            def _():
                to_far_relay(j, i, ref).start()

            @pl.when(jnp.logical_not(around))
            def _():
                along_z(j, i, ref).start()
        else:
            along_z(j, i, ref).start()

    def stage_a(j):
        @pl.when(off)
        def _():
            for i in (1, 3, 2):
                to_relay(j, i).start()

        @pl.when(diag & moves)
        def _():
            for i in (1, 3, 0, 2):
                start_z(j, i, rows(j, i))

        @pl.when(diag & stays)
        def _():
            for i in range(4):
                local_piece(j, i).start()

    def stage_b(j):
        def go(i):
            @pl.when(stays)
            def _():
                step_across(j, i, True).start()

            @pl.when(moves)
            def _():
                step_across(j, i, False).start()

        @pl.when(off)
        def _():
            go(0)

        for i in (1, 3, 2):

            @pl.when(relays(i))
            def _():
                landed(ybuf.at[j, i - 1], r_y.at[j, i - 1])
                go(i)

    def stage_c(j):
        @pl.when(off & moves)
        def _():
            for i in (0, 1, 3, 2):
                landed(turned.at[j, i], r_t.at[j, i])
                start_z(j, i, turned.at[j, i])

    def stage_w(j):
        for e in range(2):

            @pl.when(w_ends[e][0])
            def _():
                for i in LONG:
                    landed(wbuf.at[j, i // 2, e], r_w.at[j, i // 2, e])
                    from_far_relay(j, i, e).start()

    stage_a(0)
    stage_a(1)

    for d in range(3):
        send(field.at[:, :, src], field.at[:, :, src], s_f1.at[d], r_f1.at[d], zl_peers[d]).wait_recv()
    mine_y = field.at[:, :, pl.ds(4 * y, 4)]
    f2 = [send(mine_y, mine_y, s_f2.at[d], r_f2.at[d], y_peers[d]) for d in range(3)]
    for cp in f2:
        cp.start()
    for cp in f2:
        cp.wait_recv()
    f3 = send(field, field_b, s_f3, r_f3, partner)
    f3.start()
    for cp in local:
        cp.wait()

    def make_front(b, field, half):
        def for_op(k, carry):
            gamma = gam[k]
            m_re = field[k, 0].astype(F32).reshape(128, 128)
            m_im = field[k, 1].astype(F32).reshape(128, 128)
            for t in range(4):
                spin = tab[gamma * 4 + t]
                g_re = tab[64 + gamma * 4 + t].astype(F32)
                g_im = tab[128 + gamma * 4 + t].astype(F32)
                top = (g_re * m_re - g_im * m_im).astype(BF)
                low = (g_re * m_im + g_im * m_re).astype(BF)
                mix = jnp.concatenate(
                    [jnp.concatenate([top, low], axis=1), jnp.concatenate([-low, top], axis=1)], axis=0
                )
                left = jnp.concatenate(
                    [half[0, spin].reshape(256, 128), half[1, spin].reshape(256, 128)], axis=1
                )
                made = jnp.dot(left, mix, preferred_element_type=F32).astype(BF)
                made = made.reshape(4, 2, 32, 256)
                front[b, 0, :, :, k, :, t * 128 : (t + 1) * 128] = made[..., :128]
                front[b, 1, :, :, k, :, t * 128 : (t + 1) * 128] = made[..., 128:]
            return carry

        lax.fori_loop(0, 4, for_op, 0)

    stage_b(0)
    stage_a(2)
    make_front(0, field, half)
    stage_c(0)
    stage_b(1)
    stage_a(3)
    f3.wait_recv()
    for cp in swap:
        cp.wait_recv()
    make_front(1, field_b, half_b)
    stage_c(1)
    stage_b(2)
    stage_w(0)
    def x_copy(j, d):
        return send(xs.at[j, d], xr.at[j, d], s_x.at[j, d], r_x.at[j, d], x_peers[d])

    def z_copy(j):
        return send(zs.at[j], zr.at[j], s_z.at[j], r_z.at[j], z_peer)

    def product(j):
        for b in (0, 1):
            re = mir[b, j, :, 0].reshape(128, 512)
            im = mir[b, j, :, 1].reshape(128, 512)
            if j >= 2:
                re, im = -re, -im
            turn[b, 0] = jnp.concatenate([re, -im], axis=0).T
            turn[b, 1] = jnp.concatenate([im, re], axis=0).T

        def part(row):
            total = jnp.zeros((256, 256), F32)
            for b in (0, 1):
                for p in (0, 1):
                    total += jnp.dot(
                        front[b, p, row].reshape(256, 512), turn[b, p], preferred_element_type=F32
                    )
            return total

        for d in (1, 0, 2):
            xs[j, d] = part((x + d + 1) % 4).astype(BF)
            x_copy(j, d).start()
        mine[j] = part(x)

    def over_x(j):
        for d in range(3):
            x_copy(j, d).wait_recv()

        def rows_of(which):
            at = pl.ds(pl.multiple_of(which * 128, 128), 128)
            total = mine[j, at]
            for d in range(3):
                total += xr[j, d, at].astype(F32)
            return total

        zs[j] = rows_of(1 - zh).astype(BF)
        z_copy(j).start()
        keep[j] = rows_of(zh)

    def over_z(j):
        z_copy(j).wait_recv()
        total = (keep[j] + zr[j].astype(F32)).reshape(4, 32, 256)
        for p in (0, 1):
            out[:, p, :, j * 128 : (j + 1) * 128] = total[..., p * 128 : (p + 1) * 128]

    def fwd(j, q):
        return send(mir.at[0, j, q], mir.at[1, j, q], s_fwd.at[j, q], r_fwd.at[j, q], partner)

    def arrive(j):
        for q in (0, 2, 1, 3):
            local_piece(j, q).wait()
            fwd(j, q).start()

    for j in range(CHUNKS):
        arrive(j)
        if j == 0:
            stage_b(3)
            stage_c(2)
        if j == 1:
            stage_c(3)
        for q in (0, 2, 1, 3):
            fwd(j, q).wait_recv()
        product(j)
        if j + 1 < CHUNKS:
            stage_w(j + 1)
        if j >= 1:
            over_x(j - 1)
        if j >= 2:
            over_z(j - 2)
    over_x(CHUNKS - 1)
    over_z(CHUNKS - 2)
    over_z(CHUNKS - 1)

    for cp in [*f1, *f2, f3, *swap]:
        cp.wait_send()

    for j in range(CHUNKS):

        @pl.when(off)
        def _():
            step_across(j, 0, False).wait_send()
            for i in (1, 2, 3):
                to_relay(j, i).wait_send()

        @pl.when(moves)
        def _():
            for i in range(4):
                along_z(j, i, turned.at[j, i]).wait_send()

        for i in (1, 2, 3):

            @pl.when(relays(i))
            def _():
                step_across(j, i, False).wait_send()

        for e in range(2):

            @pl.when(w_ends[e][0])
            def _():
                for i in LONG:
                    from_far_relay(j, i, e).wait_send()

        for q in range(4):
            fwd(j, q).wait_send()
        for d in range(3):
            x_copy(j, d).wait_send()
        z_copy(j).wait_send()


def on_device(perambulator, meson_field, op_momentum, op_gamma):
    tau = perambulator.reshape(2, 8, 2, 32, 512)
    tab = jnp.asarray(spin_table())
    vmem = pl.BlockSpec(memory_space=pltpu.VMEM)
    dma = pltpu.SemaphoreType.DMA
    loops = pl.pallas_call(
        kernel,
        out_shape=jax.ShapeDtypeStruct((4, 2, 32, 512), F32),
        in_specs=[pl.BlockSpec(memory_space=pl.ANY)] * 5,
        out_specs=vmem,
        scratch_shapes=[
            pltpu.SMEM((4,), jnp.int32),
            pltpu.SMEM((4,), jnp.int32),
            pltpu.SMEM((192,), jnp.int32),
            pltpu.VMEM((1, 27, 2, 8, 128), BF),
            pltpu.VMEM((4, 2, 16, 8, 128), BF),
            pltpu.VMEM((4, 2, 16, 8, 128), BF),
            pltpu.VMEM((2, 4, 8, 32, 128), BF),
            pltpu.VMEM((2, 4, 8, 32, 128), BF),
            pltpu.VMEM((2, CHUNKS, 4, 2, 32, 512), BF),
            pltpu.VMEM((2, 2, 4, 2, 4, 32, 512), BF),
            pltpu.VMEM((2, 2, 512, 256), BF),
            pltpu.VMEM((CHUNKS, 256, 256), F32),
            pltpu.VMEM((CHUNKS, 3, 256, 256), BF),
            pltpu.VMEM((CHUNKS, 3, 256, 256), BF),
            pltpu.VMEM((CHUNKS, 128, 256), F32),
            pltpu.VMEM((CHUNKS, 128, 256), BF),
            pltpu.VMEM((CHUNKS, 128, 256), BF),
            pltpu.VMEM((CHUNKS, 3, 2, 32, 512), BF),
            pltpu.VMEM((CHUNKS, 2, 2, 2, 32, 512), BF),
            pltpu.VMEM((CHUNKS, 4, 2, 32, 512), BF),
            dma((2, 4)), dma((2, 4)), dma((2, 4)), dma((3,)), dma((3,)), dma((3,)), dma((3,)), dma(()), dma(()),
            dma((CHUNKS, 4)), dma((CHUNKS, 4)), dma((CHUNKS, 4)), dma((CHUNKS, 4)),
            dma((CHUNKS, 3)), dma((CHUNKS, 3)), dma((CHUNKS,)), dma((CHUNKS,)),
            dma((CHUNKS, 3)), dma((CHUNKS, 3)), dma((CHUNKS, 2, 2)), dma((CHUNKS, 2, 2)), dma((CHUNKS, 4)), dma((CHUNKS, 4)),
        ],
        compiler_params=pltpu.CompilerParams(
            collective_id=0, has_side_effects=True, vmem_limit_bytes=66_200_000
        ),
        name="loops",
    )(op_gamma, op_momentum, tab, tau, meson_field)
    return jnp.transpose(loops, (2, 0, 1, 3)).reshape(32, 1, 4, 2, 512)


def solution(mesh):
    return jax.shard_map(
        on_device,
        mesh=mesh,
        in_specs=(P("src", "snk"), P("snk", None, None, "src"), P(), P()),
        out_specs=P("snk", "src"),
        check_vma=False,
    )
```

```python
import jax
import jax.numpy as jnp
import numpy as np
from jax import lax
from jax.experimental import pallas as pl
from jax.experimental.pallas import tpu as pltpu
from jax.sharding import PartitionSpec as P

MESH = pl.DeviceIdType.MESH
NX, NY, NZ = 4, 4, 8
CHUNKS = 4
LONG = (1, 3)
BF, F32 = jnp.bfloat16, jnp.float32


def gamma_table():
    zero = np.zeros((4, 4))
    basis = [
        (zero, np.array([[0, 0, 0, 1], [0, 0, 1, 0], [0, -1, 0, 0], [-1, 0, 0, 0]], dtype=float)),
        (np.array([[0, 0, 0, -1], [0, 0, 1, 0], [0, 1, 0, 0], [-1, 0, 0, 0]], dtype=float), zero),
        (zero, np.array([[0, 0, 1, 0], [0, 0, 0, -1], [-1, 0, 0, 0], [0, 1, 0, 0]], dtype=float)),
        (np.array([[0, 0, 1, 0], [0, 0, 0, 1], [1, 0, 0, 0], [0, 1, 0, 0]], dtype=float), zero),
    ]
    table = []
    for number in range(16):
        mat = np.eye(4, dtype=complex)
        for bit in range(4):
            if number >> bit & 1:
                mat = mat @ (basis[bit][0] + 1j * basis[bit][1])
        table.append(mat)
    return np.stack(table)


def spin_table():
    table = gamma_table()
    g5 = np.real(np.diagonal(table[15]))
    rows = np.argmax(np.abs(table), axis=1)
    entry = np.take_along_axis(table, rows[:, None, :], axis=1)[:, 0, :] * g5[None, :]
    flat = np.stack([rows, np.real(entry), np.imag(entry)]).round().astype(np.int32)
    return flat.reshape(3 * 64)


def place(x, y, z, c):
    return (y * 4 + z % 4, x * 4 + (z // 4) * 2 + c)


def goes_around(z, c):
    return (z == 2) | (z == 5) | ((z == 3) & (c == 1)) | ((z == 4) & (c == 0))


def kernel(gam_in, mom_in, tab_in, tau, mes_in, out, gam, mom, tab, mes, field, field_b, half, half_b, mir, front, turn, mine, xs, xr, keep, zs, zr, ybuf, wbuf, turned,
           s_loc, s_half, r_half, s_f1, r_f1, s_f2, r_f2, s_f3, r_f3, s_mir, r_mir, s_fwd, r_fwd,
           s_x, r_x, s_z, r_z, s_y, r_y, s_w, r_w, s_t, r_t):
    src, snk = lax.axis_index("src"), lax.axis_index("snk")
    x, y, zh, zl, c = snk // 4, src // 4, (snk // 2) % 2, src % 4, snk % 2
    z = zh * 4 + zl
    l1, l0 = zl // 2, zl % 2
    other = 1 - c
    partner = place(x, y, z, other)
    zm, cm = l1 * 4 + zh * 2 + c, l0
    across = place(y, x, z, c)
    around, around_in = goes_around(z, c), goes_around(zm, cm)
    end = (z == 0) | (z == 7)
    end_two = ((z == 7) & (c == 0)) | ((z == 0) & (c == 1))
    w_slot = jnp.where((z == 2) | (z == 5), 0, 1)
    up = z == 7
    w_ends = (
        (end, place(x, y, jnp.where(up, 2, 5), c), place(x, y, jnp.where(up, 4 + c, 2 + c), jnp.where(up, 0, 1))),
        (end_two, place(x, y, jnp.where(up, 4, 3), c), place(x, y, jnp.where(up, 2, 5), jnp.where(up, 0, 1))),
    )
    diag, off = x == y, x != y
    stays = (z == zm) & (c == cm)
    moves = jnp.logical_not(stays)
    z_mirror = place(x, y, zm, cm)
    far_relay = place(x, y, 7 * (1 - z % 2), c)
    far_relay_in = place(x, y, 7 * (1 - zm % 2), cm)

    def behind(i):
        return (y + 4 - i) % 4

    def relays(i):
        return x != behind(i)

    zl_peers = [place(x, y, zh * 4 + (zl + d) % 4, c) for d in (1, 2, 3)]
    y_peers = [place(x, (y + d) % 4, z, c) for d in (1, 2, 3)]
    x_peers = [place((x + d) % 4, y, z, c) for d in (1, 2, 3)]
    z_peer = place(x, y, (z + 4) % 8, c)

    pltpu.make_async_copy(mes_in, mes, s_loc.at[1, 3]).start()
    pltpu.make_async_copy(gam_in, gam, s_loc.at[0, 0]).start()
    pltpu.make_async_copy(mom_in, mom, s_loc.at[0, 1]).start()
    pltpu.make_async_copy(tab_in, tab, s_loc.at[0, 2]).start()
    bar = pltpu.get_barrier_semaphore()
    for dev in [partner, z_peer, *zl_peers, *y_peers, *x_peers]:
        pl.semaphore_signal(bar, inc=1, device_id=dev, device_id_type=MESH)

    def greet(cond, *devs):
        @pl.when(cond)
        def _():
            for dev in devs:
                pl.semaphore_signal(bar, inc=1, device_id=dev, device_id_type=MESH)

        return jnp.where(cond, len(devs), 0)

    peers = 11
    peers += greet(off, across)
    for i in (1, 2, 3):
        peers += greet(relays(i), place(behind(i), x, z, c))
        peers += greet(off, place(y, (x + i) % 4, z, c))
    peers += greet(moves, z_mirror)
    peers += greet(around, far_relay)
    peers += greet(around_in, far_relay_in)
    for cond, dev_from, dev_to in w_ends:
        peers += greet(cond, dev_from, dev_to)

    pltpu.make_async_copy(mes_in, mes, s_loc.at[1, 3]).wait()
    pltpu.make_async_copy(gam_in, gam, s_loc.at[0, 0]).wait()
    pltpu.make_async_copy(mom_in, mom, s_loc.at[0, 1]).wait()
    pltpu.make_async_copy(tab_in, tab, s_loc.at[0, 2]).wait()
    for k in range(4):
        field[k, :, src] = mes[0, mom[k]]
    local = [
        pltpu.make_async_copy(
            tau.at[p, :, c, :, s * 128 : (s + 1) * 128], half.at[p, s], s_loc.at[p, s]
        )
        for p in range(2)
        for s in range(4)
    ]
    for cp in local:
        cp.start()

    pl.semaphore_wait(bar, peers)

    def send(a, b, ss, rs, dev):
        return pltpu.make_async_remote_copy(
            src_ref=a, dst_ref=b, send_sem=ss, recv_sem=rs, device_id=dev, device_id_type=MESH
        )

    f1 = [
        send(field.at[:, :, src], field.at[:, :, src], s_f1.at[d], r_f1.at[d], zl_peers[d])
        for d in range(3)
    ]
    for cp in f1:
        cp.start()
    swap = [
        send(
            tau.at[p, :, other, :, s * 128 : (s + 1) * 128],
            half_b.at[p, s],
            s_half.at[p, s],
            r_half.at[p, s],
            partner,
        )
        for p in range(2)
        for s in range(4)
    ]
    for cp in swap:
        cp.start()
    def rows(j, i):
        return tau.at[:, 2 * j + i // 2, i % 2]

    def landed(ref, sem):
        pltpu.make_async_copy(ref, ref, sem).wait()

    def to_relay(j, i):
        dev = place(x, (y + i) % 4, z, c)
        return send(rows(j, i), ybuf.at[j, i - 1], s_mir.at[j, i], r_y.at[j, i - 1], dev)

    def step_across(j, i, final):
        dst, sem = (mir.at[0, j, i], r_mir.at[j, i]) if final else (turned.at[j, i], r_t.at[j, i])
        if i == 0:
            return send(rows(j, 0), dst, s_mir.at[j, 0], sem, across)
        dev = place(behind(i), x, z, c)
        return send(ybuf.at[j, i - 1], dst, s_y.at[j, i - 1], sem, dev)

    def along_z(j, i, ref):
        return send(ref, mir.at[0, j, i], s_t.at[j, i], r_mir.at[j, i], z_mirror)

    def to_far_relay(j, i, ref):
        return send(ref, wbuf.at[j, i // 2, w_slot], s_t.at[j, i], r_w.at[j, i // 2, w_slot], far_relay)

    def from_far_relay(j, i, e):
        k = i // 2
        return send(wbuf.at[j, k, e], mir.at[0, j, i], s_w.at[j, k, e], r_mir.at[j, i], w_ends[e][2])

    def local_piece(j, i):
        return pltpu.make_async_copy(rows(j, i), mir.at[0, j, i], r_mir.at[j, i])

    def start_z(j, i, ref):
        if i in LONG:

            @pl.when(around)
            def _():
                to_far_relay(j, i, ref).start()

            @pl.when(jnp.logical_not(around))
            def _():
                along_z(j, i, ref).start()
        else:
            along_z(j, i, ref).start()

    def stage_a(j):
        @pl.when(off)
        def _():
            for i in (1, 3, 2):
                to_relay(j, i).start()

        @pl.when(diag & moves)
        def _():
            for i in (1, 3, 0, 2):
                start_z(j, i, rows(j, i))

        @pl.when(diag & stays)
        def _():
            for i in range(4):
                local_piece(j, i).start()

    def stage_b(j):
        def go(i):
            @pl.when(stays)
            def _():
                step_across(j, i, True).start()

            @pl.when(moves)
            def _():
                step_across(j, i, False).start()

        @pl.when(off)
        def _():
            go(0)

        for i in (1, 3, 2):

            @pl.when(relays(i))
            def _():
                landed(ybuf.at[j, i - 1], r_y.at[j, i - 1])
                go(i)

    def stage_c(j):
        @pl.when(off & moves)
        def _():
            for i in (0, 1, 3, 2):
                landed(turned.at[j, i], r_t.at[j, i])
                start_z(j, i, turned.at[j, i])

    def stage_w(j):
        for e in range(2):

            @pl.when(w_ends[e][0])
            def _():
                for i in LONG:
                    landed(wbuf.at[j, i // 2, e], r_w.at[j, i // 2, e])
                    from_far_relay(j, i, e).start()

    stage_a(0)
    stage_a(1)


    def make_front(b, field, half):
        def for_op(k, carry):
            gamma = gam[k]
            m_re = field[k, 0].astype(F32).reshape(128, 128)
            m_im = field[k, 1].astype(F32).reshape(128, 128)
            for t in range(4):
                spin = tab[gamma * 4 + t]
                g_re = tab[64 + gamma * 4 + t].astype(F32)
                g_im = tab[128 + gamma * 4 + t].astype(F32)
                top = (g_re * m_re - g_im * m_im).astype(BF)
                low = (g_re * m_im + g_im * m_re).astype(BF)
                mix = jnp.concatenate(
                    [jnp.concatenate([top, low], axis=1), jnp.concatenate([-low, top], axis=1)], axis=0
                )
                left = jnp.concatenate(
                    [half[0, spin].reshape(256, 128), half[1, spin].reshape(256, 128)], axis=1
                )
                made = jnp.dot(left, mix, preferred_element_type=F32).astype(BF)
                made = made.reshape(4, 2, 32, 256)
                front[b, 0, :, :, k, :, t * 128 : (t + 1) * 128] = made[..., :128]
                front[b, 1, :, :, k, :, t * 128 : (t + 1) * 128] = made[..., 128:]
            return carry

        lax.fori_loop(0, 4, for_op, 0)

    for d in range(3):
        send(field.at[:, :, src], field.at[:, :, src], s_f1.at[d], r_f1.at[d], zl_peers[d]).wait_recv()
    mine_y = field.at[:, :, pl.ds(4 * y, 4)]
    f2 = [send(mine_y, mine_y, s_f2.at[d], r_f2.at[d], y_peers[d]) for d in range(3)]
    for cp in f2:
        cp.start()
    stage_b(0)
    stage_a(2)
    for cp in f2:
        cp.wait_recv()
    f3 = send(field, field_b, s_f3, r_f3, partner)
    f3.start()
    stage_c(0)
    for cp in local:
        cp.wait()
    make_front(0, field, half)
    stage_b(1)
    stage_a(3)
    f3.wait_recv()
    for cp in swap:
        cp.wait_recv()
    make_front(1, field_b, half_b)
    stage_c(1)
    stage_b(2)
    stage_w(0)
    def x_copy(j, d):
        return send(xs.at[j, d], xr.at[j, d], s_x.at[j, d], r_x.at[j, d], x_peers[d])

    def z_copy(j):
        return send(zs.at[j], zr.at[j], s_z.at[j], r_z.at[j], z_peer)

    def product(j):
        for b in (0, 1):
            re = mir[b, j, :, 0].reshape(128, 512)
            im = mir[b, j, :, 1].reshape(128, 512)
            if j >= 2:
                re, im = -re, -im
            turn[b, 0] = jnp.concatenate([re, -im], axis=0).T
            turn[b, 1] = jnp.concatenate([im, re], axis=0).T

        def part(row):
            total = jnp.zeros((256, 256), F32)
            for b in (0, 1):
                for p in (0, 1):
                    total += jnp.dot(
                        front[b, p, row].reshape(256, 512), turn[b, p], preferred_element_type=F32
                    )
            return total

        for d in (1, 0, 2):
            xs[j, d] = part((x + d + 1) % 4).astype(BF)
            x_copy(j, d).start()
        mine[j] = part(x)

    def over_x(j):
        for d in range(3):
            x_copy(j, d).wait_recv()

        def rows_of(which):
            at = pl.ds(pl.multiple_of(which * 128, 128), 128)
            total = mine[j, at]
            for d in range(3):
                total += xr[j, d, at].astype(F32)
            return total

        zs[j] = rows_of(1 - zh).astype(BF)
        z_copy(j).start()
        keep[j] = rows_of(zh)

    def over_z(j):
        z_copy(j).wait_recv()
        total = (keep[j] + zr[j].astype(F32)).reshape(4, 32, 256)
        for p in (0, 1):
            out[:, p, :, j * 128 : (j + 1) * 128] = total[..., p * 128 : (p + 1) * 128]

    def fwd(j, q):
        return send(mir.at[0, j, q], mir.at[1, j, q], s_fwd.at[j, q], r_fwd.at[j, q], partner)

    def arrive(j):
        for q in (0, 2, 1, 3):
            local_piece(j, q).wait()
            fwd(j, q).start()

    for j in range(CHUNKS):
        arrive(j)
        if j == 0:
            stage_b(3)
            stage_c(2)
        if j == 1:
            stage_c(3)
        for q in (0, 2, 1, 3):
            fwd(j, q).wait_recv()
        product(j)
        if j + 1 < CHUNKS:
            stage_w(j + 1)
        if j >= 1:
            over_x(j - 1)
        if j >= 2:
            over_z(j - 2)
    over_x(CHUNKS - 1)
    over_z(CHUNKS - 2)
    over_z(CHUNKS - 1)

    for cp in [*f1, *f2, f3, *swap]:
        cp.wait_send()

    for j in range(CHUNKS):

        @pl.when(off)
        def _():
            step_across(j, 0, False).wait_send()
            for i in (1, 2, 3):
                to_relay(j, i).wait_send()

        @pl.when(moves)
        def _():
            for i in range(4):
                along_z(j, i, turned.at[j, i]).wait_send()

        for i in (1, 2, 3):

            @pl.when(relays(i))
            def _():
                step_across(j, i, False).wait_send()

        for e in range(2):

            @pl.when(w_ends[e][0])
            def _():
                for i in LONG:
                    from_far_relay(j, i, e).wait_send()

        for q in range(4):
            fwd(j, q).wait_send()
        for d in range(3):
            x_copy(j, d).wait_send()
        z_copy(j).wait_send()


def on_device(perambulator, meson_field, op_momentum, op_gamma):
    tau = perambulator.reshape(2, 8, 2, 32, 512)
    tab = jnp.asarray(spin_table())
    vmem = pl.BlockSpec(memory_space=pltpu.VMEM)
    dma = pltpu.SemaphoreType.DMA
    loops = pl.pallas_call(
        kernel,
        out_shape=jax.ShapeDtypeStruct((4, 2, 32, 512), F32),
        in_specs=[pl.BlockSpec(memory_space=pl.ANY)] * 5,
        out_specs=vmem,
        scratch_shapes=[
            pltpu.SMEM((4,), jnp.int32),
            pltpu.SMEM((4,), jnp.int32),
            pltpu.SMEM((192,), jnp.int32),
            pltpu.VMEM((1, 27, 2, 8, 128), BF),
            pltpu.VMEM((4, 2, 16, 8, 128), BF),
            pltpu.VMEM((4, 2, 16, 8, 128), BF),
            pltpu.VMEM((2, 4, 8, 32, 128), BF),
            pltpu.VMEM((2, 4, 8, 32, 128), BF),
            pltpu.VMEM((2, CHUNKS, 4, 2, 32, 512), BF),
            pltpu.VMEM((2, 2, 4, 2, 4, 32, 512), BF),
            pltpu.VMEM((2, 2, 512, 256), BF),
            pltpu.VMEM((CHUNKS, 256, 256), F32),
            pltpu.VMEM((CHUNKS, 3, 256, 256), BF),
            pltpu.VMEM((CHUNKS, 3, 256, 256), BF),
            pltpu.VMEM((CHUNKS, 128, 256), F32),
            pltpu.VMEM((CHUNKS, 128, 256), BF),
            pltpu.VMEM((CHUNKS, 128, 256), BF),
            pltpu.VMEM((CHUNKS, 3, 2, 32, 512), BF),
            pltpu.VMEM((CHUNKS, 2, 2, 2, 32, 512), BF),
            pltpu.VMEM((CHUNKS, 4, 2, 32, 512), BF),
            dma((2, 4)), dma((2, 4)), dma((2, 4)), dma((3,)), dma((3,)), dma((3,)), dma((3,)), dma(()), dma(()),
            dma((CHUNKS, 4)), dma((CHUNKS, 4)), dma((CHUNKS, 4)), dma((CHUNKS, 4)),
            dma((CHUNKS, 3)), dma((CHUNKS, 3)), dma((CHUNKS,)), dma((CHUNKS,)),
            dma((CHUNKS, 3)), dma((CHUNKS, 3)), dma((CHUNKS, 2, 2)), dma((CHUNKS, 2, 2)), dma((CHUNKS, 4)), dma((CHUNKS, 4)),
        ],
        compiler_params=pltpu.CompilerParams(
            collective_id=0, has_side_effects=True, vmem_limit_bytes=66_200_000
        ),
        name="loops",
    )(op_gamma, op_momentum, tab, tau, meson_field)
    return jnp.transpose(loops, (2, 0, 1, 3)).reshape(32, 1, 4, 2, 512)


def solution(mesh):
    return jax.shard_map(
        on_device,
        mesh=mesh,
        in_specs=(P("src", "snk"), P("snk", None, None, "src"), P(), P()),
        out_specs=P("snk", "src"),
        check_vma=False,
    )
```
